128 devices in a mesh: space: 32 (over x, y, core), member: 4 (over z).
Axes of the slice: x: 4, y: 4, z: 4, core: 2. Of those that a mesh axis runs over, the one named last changes fastest.
Arguments:
- latent: bfloat16 [16, 16384, 1024], P('member', 'space'), may hold values from -6 to 6
- w_in: bfloat16 [1024, 1024], replicated, may hold values from -0.1875 to 0.1875
- b_in: float32 [1024], replicated, may hold values from -3 to 3
- w_out: bfloat16 [1024, 96], replicated, may hold values from -0.1875 to 0.1875
- b_out: float32 [96], replicated, may hold values from -3 to 3
- target: float32 [16384, 96], P('space'), may hold values from -6 to 6
- area: float32 [16384], P('space'), may hold values from 0.5 to 40, as said below
- cell_of: int32 [16384], P('space'), may hold values from 0 to 1023, as said below
Outputs:
- latent_grad: bfloat16 [16, 16384, 1024], P('member', 'space')
- scores: float32 [2], replicated
The draws below stay inside these ranges and needn't reach their ends.
Inputs may be any that keep to these rules, and one draw needn't show every extreme that they name: `cell_of`: every node lies in one coarse cell; some cells hold no node. Positive area of each node.
All inputs are finite; a program needn't handle non-finite values.
Results may differ from the reference program's by a relative error of at most 0.03.
Values may be sent and summed in bfloat16 or wider, within the bound.
No kernel may reach another device: no remote copies, remote signals or barrier semaphores. Data moves between devices by JAX's collectives and lax.ppermute only.
A program may use at most 64 MiB of HBM per device.

```python
import jax
import jax.numpy as jnp
from jax import lax

D = 1024
UNITS = 1024
VARS = 96
NODE_DEV = 512
CELL_DEV = 32
MEMBERS = 16
NODES = 16384
CELLS = 1024
N_SPACE = 32


def draw_area(key, part):
    first = jax.random.fold_in(key, 11)
    position = jnp.arange(NODES, dtype=jnp.float32) / NODES
    ramp = jnp.exp(jnp.log(6.0) * position)
    noise = jnp.exp(jax.random.uniform(first, (NODES,), jnp.float32, jnp.log(0.5), jnp.log(2.0)))
    return ramp * noise


def draw_cell_of(key, part):
    first = jax.random.fold_in(key, 21)
    second = jax.random.fold_in(key, 22)
    third = jax.random.fold_in(key, 23)
    dense = CELLS // 8
    used = CELLS - CELLS // 8
    region = jax.random.randint(first, (NODES,), 0, 2, dtype=jnp.int32)
    in_dense = jax.random.randint(second, (NODES,), 0, dense, dtype=jnp.int32)
    in_sparse = jax.random.randint(third, (NODES,), dense, used, dtype=jnp.int32)
    return jnp.where(region == 0, in_dense, in_sparse)


def block_levels(stream_key, extent, pieces, smallest, high):
    level, own = 1.0, jax.random.fold_in(stream_key, 6)
    for dim, blocks in pieces:
        draws = jnp.exp(jax.random.uniform(jax.random.fold_in(own, dim), (blocks,), jnp.float32, smallest / len(pieces), high / len(pieces)))
        level = level * jnp.repeat(draws, extent[dim] // blocks).reshape([-1 if axis == dim else 1 for axis in range(len(extent))])
    return level


def bell_draw(rng, extent, spread, limit, split=(), kind=jnp.bfloat16):
    drawn = spread * jax.random.normal(rng, extent, jnp.float32)
    if split:
        drawn = drawn * block_levels(rng, extent, split, -0.22, 0.18)
    return jnp.clip(drawn, -limit, limit).astype(kind)


def setup_inputs(seed: int = 0) -> dict:
    splits = jax.random.split(jax.random.key(seed), 9)
    latent = bell_draw(splits[0], (MEMBERS, NODES, D), 1.0, 6.0, ((0, 4), (1, 32)))
    w_in = bell_draw(splits[1], (D, UNITS), D ** -0.5, 0.1875)
    b_in = bell_draw(splits[2], (UNITS,), 0.5, 3.0, (), jnp.float32)
    w_out = bell_draw(splits[3], (UNITS, VARS), UNITS ** -0.5, 0.1875)
    b_out = bell_draw(splits[4], (VARS,), 0.5, 3.0, (), jnp.float32)
    target = bell_draw(splits[5], (NODES, VARS), 1.0, 6.0, ((0, 32),), jnp.float32)
    area = draw_area(jax.random.fold_in(splits[8], 71), 0)
    cell_of = draw_cell_of(jax.random.fold_in(splits[8], 71), 0)
    return dict(latent=latent, w_in=w_in, b_in=b_in, w_out=w_out, b_out=b_out, target=target, area=area, cell_of=cell_of)


epsilon = 1e-05
loss_scale = 4096.0

def silu_slope(preact):
    sigma = jax.nn.sigmoid(preact)
    return sigma * (1.0 + preact * (1.0 - sigma))

def energy(own_part, everyone, truths, weight, own_ids):
    members = everyone.shape[0]
    variables = everyone.shape[1]
    to_truth = own_part - truths[None]
    truth_dist = jnp.sqrt(lax.optimization_barrier(jnp.mean(to_truth * to_truth, axis=1)) + epsilon)
    between = own_part[:, None] - everyone[None]
    pair_dist = jnp.sqrt(lax.optimization_barrier(jnp.mean(between * between, axis=2)) + epsilon)
    distinct = (own_ids[:, None] != jnp.arange(members, dtype=jnp.int32)[None]).astype(own_part.dtype)
    pair_weight = distinct[:, :, None] / pair_dist
    node_loss = weight * (lax.optimization_barrier(jnp.sum(truth_dist, axis=0)) / members - lax.optimization_barrier(jnp.sum(distinct[:, :, None] * pair_dist, axis=(0, 1))) / (2.0 * members * (members - 1)))
    gradient = weight * (to_truth / truth_dist[:, None] / (members * variables) - lax.optimization_barrier(jnp.sum(between * pair_weight[:, :, None], axis=1)) / (members * (members - 1) * variables))
    return (node_loss, gradient)

def reference(latent, w_in, b_in, w_out, b_out, target, area, cell_of):
    members, node_total, latent_width = latent.shape
    variables = w_out.shape[1]

    def forward(member_rows):
        preact = jnp.dot(member_rows, w_in, preferred_element_type=jnp.float32) + b_in
        activation = jax.nn.silu(preact).astype(jnp.bfloat16)
        return (jnp.dot(activation, w_out, preferred_element_type=jnp.float32) + b_out).astype(jnp.bfloat16)
    predictions = lax.map(forward, latent)
    pred_float = predictions.astype(jnp.float32)
    blocks = node_total // NODE_DEV
    blocked = pred_float.reshape(members, blocks, NODE_DEV, variables).transpose(1, 0, 3, 2)
    truth_blocks = target.reshape(blocks, NODE_DEV, variables).transpose(0, 2, 1)
    area_blocks = area.reshape(blocks, NODE_DEV)
    member_ids = jnp.arange(members, dtype=jnp.int32)

    def fine_block(inputs):
        own_part, truths, weight = inputs
        return energy(own_part, own_part, truths, weight, member_ids)
    fine_loss, fine_grad = lax.map(fine_block, (blocked, truth_blocks, area_blocks))
    fine_node = lax.optimization_barrier(fine_grad.astype(jnp.bfloat16))
    fine_node = fine_node.transpose(1, 0, 3, 2).reshape(members, node_total, variables)
    cells = CELL_DEV * N_SPACE
    flattened = pred_float.transpose(1, 0, 2).reshape(node_total, members * variables)
    cell_sum = jax.ops.segment_sum(flattened, cell_of, cells)
    counts = jax.ops.segment_sum(jnp.ones((node_total,), jnp.float32), cell_of, cells)
    cell_area = jax.ops.segment_sum(area, cell_of, cells)
    target_sum = jax.ops.segment_sum(target, cell_of, cells)
    divisor = jnp.maximum(counts, 1.0)
    cell_mean = lax.optimization_barrier((cell_sum / divisor[:, None]).astype(jnp.bfloat16))
    cell_mean = cell_mean.astype(jnp.float32).reshape(cells, members, variables).transpose(1, 2, 0)
    cell_target = (target_sum / divisor[:, None]).T
    coarse_loss, coarse_grad = energy(cell_mean, cell_mean, cell_target, cell_area, member_ids)
    per_cell = lax.optimization_barrier((coarse_grad / divisor[None, None, :]).astype(jnp.bfloat16))
    node_coarse = jnp.take(per_cell, cell_of, axis=2).transpose(0, 2, 1)
    upstream = (fine_node.astype(jnp.float32) + node_coarse.astype(jnp.float32)).astype(jnp.bfloat16)
    total_area = jnp.sum(area)
    factor = loss_scale * node_total / total_area

    def backward(inputs):
        member_rows, member_up = inputs
        preact = jnp.dot(member_rows, w_in, preferred_element_type=jnp.float32) + b_in
        hidden_grad = jnp.dot(member_up, w_out.T, preferred_element_type=jnp.float32)
        preact_grad = (hidden_grad * silu_slope(preact)).astype(jnp.bfloat16)
        return (jnp.dot(preact_grad, w_in.T, preferred_element_type=jnp.float32) * factor).astype(jnp.bfloat16)
    latent_grad = lax.map(backward, (latent, upstream))
    scores = jnp.stack([jnp.sum(fine_loss), jnp.sum(coarse_loss)]) / total_area
    return (latent_grad, scores)
```

```python
import functools

import jax
import jax.numpy as jnp
from jax import lax
from jax.experimental import pallas as pl
from jax.experimental.pallas import tpu as pltpu
from jax.sharding import Mesh
from jax.sharding import PartitionSpec as P

SPACE = ("x", "y", "c")
WIDE = ("x", "y", "m")

EPSILON = 1e-05
LOSS_SCALE = 4096.0
LANES = 128
VARS = 96
FOUR = 4
MEMBERS = 16
CELLS = 1024
HALF = CELLS // 2
NODE_TOTAL = 16384
PAIRS = float(MEMBERS * (MEMBERS - 1))
TRUTH_SCALE = 1.0 / (MEMBERS * VARS)
PAIR_SCALE = 1.0 / (PAIRS * VARS)

f32 = jnp.float32
bf16 = jnp.bfloat16


def vmem():
    return pl.BlockSpec(memory_space=pltpu.VMEM)


def forward_kernel(x_ref, w_ref, b_ref, wo_ref, extra_ref, preact_ref, pred_ref):
    total = extra_ref[...]
    units = w_ref.shape[1]
    step = 256
    for n in range(0, units, step):
        pre = jnp.dot(x_ref[...], w_ref[:, n : n + step], preferred_element_type=f32)
        pre = pre + b_ref[:, n : n + step]
        preact_ref[:, n : n + step] = pre
        half = 0.5 * pre
        act = (half + half * jnp.tanh(half)).astype(bf16)
        total = total + jnp.dot(act, wo_ref[n : n + step, :], preferred_element_type=f32)
    pred_ref[...] = total.astype(bf16)


def forward(flat, w_in, b_in, w_pad, extra, nodes):
    rows = 256
    tiles = nodes // rows
    width, units = w_in.shape
    return pl.pallas_call(
        forward_kernel,
        grid=(FOUR, tiles),
        in_specs=[
            pl.BlockSpec((rows, width), lambda j, t: (j * tiles + t, 0)),
            pl.BlockSpec((width, units), lambda j, t: (0, 0)),
            pl.BlockSpec((1, units), lambda j, t: (0, 0)),
            pl.BlockSpec((units, LANES), lambda j, t: (0, 0)),
            pl.BlockSpec((rows, LANES), lambda j, t: (t, j)),
        ],
        out_specs=[
            pl.BlockSpec((rows, units), lambda j, t: (j * tiles + t, 0)),
            pl.BlockSpec((rows, LANES), lambda j, t: (t, j)),
        ],
        out_shape=[
            jax.ShapeDtypeStruct((FOUR * nodes, units), f32),
            jax.ShapeDtypeStruct((nodes, FOUR * LANES), bf16),
        ],
        cost_estimate=pl.CostEstimate(
            flops=2 * FOUR * nodes * width * units, bytes_accessed=16 << 20, transcendentals=0
        ),
        name="forward",
    )(flat, w_in, b_in, w_pad, extra)


def cells_kernel(base, row_ref, pred_ref, out_ref):
    nodes = pred_ref.shape[0]
    ids = lax.broadcasted_iota(jnp.int32, (HALF, nodes), 0) + base
    picker = jnp.where(ids == row_ref[...], 1.0, 0.0).astype(bf16)
    out_ref[...] = jnp.dot(picker, pred_ref[...], preferred_element_type=f32).astype(out_ref.dtype)


def cell_sums(row, pred, base, dtype):
    return pl.pallas_call(
        functools.partial(cells_kernel, base),
        in_specs=[vmem(), vmem()],
        out_specs=vmem(),
        out_shape=jax.ShapeDtypeStruct((HALF, pred.shape[1]), dtype),
        cost_estimate=pl.CostEstimate(
            flops=2 * HALF * pred.size, bytes_accessed=2 << 20, transcendentals=0
        ),
        name="cells",
    )(row, pred)


def fine_kernel(place_ref, got_ref, truth_ref, area_ref, grad_ref, loss_ref, part, slope):
    for k in range(MEMBERS):
        block = got_ref[k // FOUR, :, (k % FOUR) * LANES : (k % FOUR + 1) * LANES]
        part[k] = block.astype(f32).T[:VARS, :]
    start = pl.multiple_of(place_ref[0] * LANES, LANES)
    truth = truth_ref[:, pl.ds(start, LANES)]
    area = area_ref[:, pl.ds(start, LANES)]
    slope[:, VARS:, :] = jnp.zeros((MEMBERS, LANES - VARS, LANES), f32)

    def member(m, carry):
        truths, pairs = carry
        own = part[m]
        off = own - truth
        mean = jnp.sum(off * off, axis=0, keepdims=True) * (1.0 / VARS) + EPSILON
        inverse = lax.rsqrt(mean)
        truths = truths + mean * inverse
        total = jnp.zeros_like(own)
        for k in range(MEMBERS):
            between = own - part[k]
            mean = jnp.sum(between * between, axis=0, keepdims=True) * (1.0 / VARS) + EPSILON
            weight = lax.rsqrt(mean)
            distinct = jnp.where(m == k, 0.0, 1.0)
            pairs = pairs + (mean * weight) * distinct
            total = total + between * weight
        slope[m, :VARS, :] = off * (inverse * area * TRUTH_SCALE) - total * (area * PAIR_SCALE)
        return truths, pairs

    zero = jnp.zeros((1, LANES), f32)
    truths, pairs = lax.fori_loop(0, MEMBERS, member, (zero, zero))
    loss_ref[...] = area * (truths * (1.0 / MEMBERS) - pairs * (0.5 / PAIRS))
    for k in range(MEMBERS):
        grad_ref[k // FOUR, :, (k % FOUR) * LANES : (k % FOUR + 1) * LANES] = slope[k].T.astype(bf16)


def fine(place, got, truth, area):
    return pl.pallas_call(
        fine_kernel,
        in_specs=[pl.BlockSpec(memory_space=pltpu.SMEM), vmem(), vmem(), vmem()],
        out_specs=[vmem(), vmem()],
        out_shape=[
            jax.ShapeDtypeStruct(got.shape, bf16),
            jax.ShapeDtypeStruct((1, LANES), f32),
        ],
        scratch_shapes=[
            pltpu.VMEM((MEMBERS, VARS, LANES), f32),
            pltpu.VMEM((MEMBERS, LANES, LANES), f32),
        ],
        cost_estimate=pl.CostEstimate(
            flops=MEMBERS * MEMBERS * VARS * LANES * 16, bytes_accessed=2 << 20, transcendentals=0
        ),
        name="fine",
    )(place, got, truth, area)


def three(value):
    high = value.astype(bf16).astype(f32)
    rest = value - high
    middle = rest.astype(bf16).astype(f32)
    return high, middle, rest - middle


def coarse_kernel(got_ref, loss_ref, area_ref, out_ref):
    places = got_ref.shape[0] // FOUR
    lane = lax.broadcasted_iota(jnp.int32, (8, LANES), 1)
    rank = lax.broadcasted_iota(jnp.int32, (8, LANES), 0)
    real = lane < VARS
    spare = lane >= VARS + 24
    sums = []
    for m in range(FOUR):
        total = got_ref[m].astype(f32)
        for s in range(1, places):
            total = total + got_ref[s * FOUR + m].astype(f32)
        sums += [total[:, j * LANES : (j + 1) * LANES] for j in range(FOUR)]

    def across(value):
        return jnp.sum(value, axis=1, keepdims=True)

    counts = across(jnp.where(spare, sums[0] + sums[1], 0.0))
    weight = across(jnp.where(spare, sums[2], 0.0))
    inverse = 1.0 / jnp.maximum(counts, 1.0)
    truth = jnp.zeros((8, LANES), f32)
    for j in range(FOUR):
        turned = pltpu.roll(sums[j], (24 * j - VARS) % LANES, 1)
        truth = jnp.where((lane >= 24 * j) & (lane < 24 * (j + 1)), turned, truth)
    truth = truth * inverse
    means = [jnp.where(real, (v * inverse).astype(bf16).astype(f32), 0.0) for v in sums]
    truths = jnp.zeros((8, 1), f32)
    pairs = jnp.zeros((8, 1), f32)
    grads = []
    for m in range(MEMBERS):
        off = means[m] - truth
        mean = across(off * off) * (1.0 / VARS) + EPSILON
        turn = lax.rsqrt(mean)
        truths = truths + mean * turn
        grads.append(off * (turn * TRUTH_SCALE))
    for m in range(MEMBERS):
        for k in range(m):
            between = means[m] - means[k]
            mean = across(between * between) * (1.0 / VARS) + EPSILON
            turn = lax.rsqrt(mean)
            pairs = pairs + mean * turn
            pull = between * (turn * PAIR_SCALE)
            grads[m] = grads[m] - pull
            grads[k] = grads[k] + pull
    loss = jnp.sum(weight * (truths * (1.0 / MEMBERS) - pairs * (1.0 / PAIRS)), axis=0, keepdims=True)
    fine_loss = across(loss_ref[...])
    area = across(area_ref[...])
    pieces = jnp.zeros((8, LANES), f32)
    for index, value in enumerate((*three(fine_loss), *three(loss), *three(area))):
        pieces = jnp.where(lane == VARS + index, value, pieces)
    pieces = jnp.where(rank == 0, pieces, 0.0)
    scale = weight * inverse
    for m in range(FOUR):
        rows = [grads[m * FOUR + j] * scale for j in range(FOUR)]
        rows[0] = rows[0] + pieces
        block = jnp.concatenate(rows, axis=1).astype(bf16)
        for s in range(places):
            out_ref[s * FOUR + m] = block


def coarse(got, loss, area):
    return pl.pallas_call(
        coarse_kernel,
        in_specs=[vmem(), vmem(), vmem()],
        out_specs=vmem(),
        out_shape=jax.ShapeDtypeStruct(got.shape, bf16),
        cost_estimate=pl.CostEstimate(flops=1 << 21, bytes_accessed=1 << 20, transcendentals=0),
        name="coarse",
    )(got, loss, area)


def picked(base, column, table):
    ids = lax.broadcasted_iota(jnp.int32, (column.shape[0], HALF), 1) + base
    wide = jnp.concatenate([column] * (HALF // LANES), axis=1)
    picker = jnp.where(ids == wide, 1.0, 0.0).astype(bf16)
    return jnp.dot(picker, table, preferred_element_type=f32)


def near_kernel(column_ref, table_ref, out_ref):
    out_ref[...] = picked(0, column_ref[...], table_ref[...])


def near(column, table):
    return pl.pallas_call(
        near_kernel,
        in_specs=[vmem(), vmem()],
        out_specs=vmem(),
        out_shape=jax.ShapeDtypeStruct((column.shape[0], table.shape[1]), f32),
        cost_estimate=pl.CostEstimate(
            flops=2 * HALF * column.shape[0] * table.shape[1], bytes_accessed=2 << 20, transcendentals=0
        ),
        name="near",
    )(column, table)


def far_kernel(column_ref, near_ref, fine_ref, own_ref, other_ref, up_ref, factor_ref, score_ref):
    total = near_ref[...] + picked(HALF, column_ref[...], other_ref[...])
    up_ref[...] = (total + fine_ref[...].astype(f32)).astype(bf16)
    sums = own_ref[:, :LANES].astype(f32) + other_ref[:, :LANES].astype(f32)
    sums = jnp.sum(sums, axis=0, keepdims=True)
    lane = lax.broadcasted_iota(jnp.int32, (1, LANES), 1)

    def of(index):
        here = (lane >= VARS + 3 * index) & (lane < VARS + 3 * index + 3)
        return jnp.sum(jnp.where(here, sums, 0.0), axis=1, keepdims=True)

    area = of(2) * (1.0 / FOUR)
    factor_ref[...] = jnp.broadcast_to(LOSS_SCALE * NODE_TOTAL / area, (1, LANES))
    score_ref[0] = (of(0) / area)[0, 0]
    score_ref[1] = (of(1) / area)[0, 0]


def far(column, near_part, fine_part, own, other):
    return pl.pallas_call(
        far_kernel,
        in_specs=[vmem()] * 5,
        out_specs=[vmem(), vmem(), pl.BlockSpec(memory_space=pltpu.SMEM)],
        out_shape=[
            jax.ShapeDtypeStruct(fine_part.shape, bf16),
            jax.ShapeDtypeStruct((1, LANES), f32),
            jax.ShapeDtypeStruct((2,), f32),
        ],
        name="far",
    )(column, near_part, fine_part, own, other)


def backward_kernel(up_ref, preact_ref, wo_ref, w_ref, factor_ref, out_ref):
    units = w_ref.shape[1]
    step = 256
    total = None
    for n in range(0, units, step):
        hidden = jnp.dot(up_ref[...], wo_ref[:, n : n + step], preferred_element_type=f32)
        pre = preact_ref[:, n : n + step]
        half = 0.5 * pre
        sigma = 0.5 * jnp.tanh(half) + 0.5
        slope = sigma * (1.0 + pre * (1.0 - sigma))
        grad = (hidden * slope).astype(bf16)
        more = lax.dot_general(
            grad, w_ref[:, n : n + step], (((1,), (1,)), ((), ())), preferred_element_type=f32
        )
        total = more if total is None else total + more
    out_ref[...] = (total * factor_ref[0:1, 0:1]).astype(bf16)


def backward(up, preact, wo_t, w_in, factor, nodes):
    rows = 256
    tiles = nodes // rows
    width, units = w_in.shape
    return pl.pallas_call(
        backward_kernel,
        grid=(FOUR, tiles),
        in_specs=[
            pl.BlockSpec((rows, LANES), lambda j, t: (t, j)),
            pl.BlockSpec((rows, units), lambda j, t: (j * tiles + t, 0)),
            pl.BlockSpec((LANES, units), lambda j, t: (0, 0)),
            pl.BlockSpec((width, units), lambda j, t: (0, 0)),
            pl.BlockSpec((1, LANES), lambda j, t: (0, 0)),
        ],
        out_specs=pl.BlockSpec((rows, width), lambda j, t: (j * tiles + t, 0)),
        out_shape=jax.ShapeDtypeStruct((FOUR * nodes, width), bf16),
        cost_estimate=pl.CostEstimate(
            flops=2 * FOUR * nodes * width * units, bytes_accessed=16 << 20, transcendentals=0
        ),
        name="backward",
    )(up, preact, wo_t, w_in, factor)


def features(target, area, nodes):
    turn = jnp.arange(nodes, dtype=jnp.int32)[:, None]
    eight = jnp.arange(8, dtype=jnp.int32)[None, :]
    low = (turn % 16 == eight).astype(f32)
    high = (turn % 16 == eight + 8).astype(f32)
    spread = jnp.where(turn % 8 == eight, area[:, None], 0.0)
    return (low, high, spread, jnp.zeros_like(spread))


def shards(latent, w_in, b_in, w_out, b_out, target, area, cell_of):
    members, nodes, width = latent.shape
    flat = latent.reshape(members * nodes, width)
    spare = LANES - VARS
    w_pad = jnp.pad(w_out, ((0, 0), (0, spare)))
    wo_t = jnp.pad(w_out.T, ((0, spare), (0, 0)))
    bias = jnp.broadcast_to(b_out[None, :], (nodes, VARS))
    last = features(target, area, nodes)
    pieces = []
    for j in range(FOUR):
        pieces += [bias, target[:, 24 * j : 24 * (j + 1)], last[j]]
    extra = jnp.concatenate(pieces, axis=1)
    cell = jnp.bitwise_xor(cell_of, lax.axis_index("c") * HALF)
    row = cell[None, :]
    column = jnp.broadcast_to(cell[:, None], (nodes, LANES))
    area_row = area[None, :]
    place = lax.axis_index("m").astype(jnp.int32)[None]

    preact, pred = forward(flat, w_in, b_in[None, :], w_pad, extra, nodes)
    swap = [(0, 1), (1, 0)]
    sent = cell_sums(row, pred, HALF, bf16)
    arrived = lax.ppermute(sent, "c", swap)
    kept = cell_sums(row, pred, 0, f32)
    both = (kept + arrived.astype(f32)).astype(bf16).reshape(64, 8, FOUR * LANES)
    gathered = lax.all_to_all(both, WIDE, 0, 0, tiled=True)
    everyone = lax.all_to_all(pred.reshape(FOUR, LANES, FOUR * LANES), "m", 0, 0, tiled=True)
    fine_grad, fine_loss = fine(place, everyone, target.T, area_row)
    table = coarse(gathered, fine_loss, area_row)
    own = lax.all_to_all(table, WIDE, 0, 0, tiled=True).reshape(HALF, FOUR * LANES)
    fine_part = lax.all_to_all(fine_grad, "m", 0, 0, tiled=True).reshape(nodes, FOUR * LANES)
    other = lax.ppermute(own, "c", swap)
    near_part = near(column, own)
    up, factor, scores = far(column, near_part, fine_part, own, other)
    latent_grad = backward(up, preact, wo_t, w_in, factor, nodes)
    return (latent_grad.reshape(members, nodes, width), scores)


def solution(mesh):
    split = Mesh(mesh.devices.reshape(4, 4, 2, mesh.shape["member"]), ("x", "y", "c", "m"))
    return jax.shard_map(
        shards,
        mesh=split,
        in_specs=(P("m", SPACE, None), P(), P(), P(), P(), P(SPACE, None), P(SPACE), P(SPACE)),
        out_specs=(P("m", SPACE, None), P()),
        check_vma=False,
    )
```

```python
import functools

import jax
import jax.numpy as jnp
from jax import lax
from jax.experimental import pallas as pl
from jax.experimental.pallas import tpu as pltpu
from jax.sharding import Mesh
from jax.sharding import PartitionSpec as P

SPACE = ("x", "y", "c")
WIDE = ("x", "y", "m")

EPSILON = 1e-05
LOSS_SCALE = 4096.0
LANES = 128
VARS = 96
FOUR = 4
MEMBERS = 16
CELLS = 1024
HALF = CELLS // 2
NODE_TOTAL = 16384
PAIRS = float(MEMBERS * (MEMBERS - 1))
TRUTH_SCALE = 1.0 / (MEMBERS * VARS)
PAIR_SCALE = 1.0 / (PAIRS * VARS)

f32 = jnp.float32
bf16 = jnp.bfloat16


def vmem():
    return pl.BlockSpec(memory_space=pltpu.VMEM)


def fits(mib):
    return pltpu.CompilerParams(vmem_limit_bytes=mib << 20)


def smem():
    return pl.BlockSpec(memory_space=pltpu.SMEM)


def forward_kernel(
    x_ref, w_ref, b_ref, wo_ref, bo_ref, truth_ref, area_ref, preact_ref, pred_ref, wide, bias, extra
):
    j = pl.program_id(0)
    nodes = x_ref.shape[0]
    spare = LANES - VARS

    @pl.when(j == 0)
    def _():
        wide[:VARS, :] = wo_ref[...]
        wide[VARS:, :] = jnp.zeros((spare, wide.shape[1]), bf16)
        bias[...] = jnp.zeros_like(bias)
        bias[:, :VARS] = bo_ref[...]
        extra[:VARS, :] = jnp.zeros((VARS, nodes), f32)

    lane = lax.broadcasted_iota(jnp.int32, (8, nodes), 1)
    rank = lax.broadcasted_iota(jnp.int32, (8, nodes), 0)
    ones = jnp.where((lane & 15) == rank + 8 * j, 1.0, 0.0)
    spread = jnp.where((lane & 7) == rank, area_ref[...], 0.0)
    extra[VARS : VARS + 24, :] = truth_ref[pl.ds(pl.multiple_of(24 * j, 8), 24), :]
    extra[VARS + 24 :, :] = jnp.where(j < 2, ones, jnp.where(j == 2, spread, 0.0))
    pre = jnp.dot(x_ref[...], w_ref[...], preferred_element_type=f32) + b_ref[...]
    preact_ref[...] = pre
    half = 0.5 * pre
    act = (half + half * jnp.tanh(half)).astype(bf16)
    total = lax.dot_general(act, wide[...], (((1,), (1,)), ((), ())), preferred_element_type=f32)
    pred_ref[...] = (total + bias[...] + extra[...].T).astype(bf16)


def forward(flat, w_in, b_in, wo_t, b_out, truth, area, nodes):
    width, units = w_in.shape
    return pl.pallas_call(
        forward_kernel,
        grid=(FOUR,),
        in_specs=[
            pl.BlockSpec((nodes, width), lambda j: (j, 0)),
            pl.BlockSpec((width, units), lambda j: (0, 0)),
            pl.BlockSpec((1, units), lambda j: (0, 0)),
            pl.BlockSpec((VARS, units), lambda j: (0, 0)),
            pl.BlockSpec((1, VARS), lambda j: (0, 0)),
            pl.BlockSpec((VARS, nodes), lambda j: (0, 0)),
            pl.BlockSpec((1, nodes), lambda j: (0, 0)),
        ],
        out_specs=[
            pl.BlockSpec((nodes, units), lambda j: (j, 0)),
            pl.BlockSpec((nodes, LANES), lambda j: (0, j)),
        ],
        out_shape=[
            jax.ShapeDtypeStruct((FOUR * nodes, units), f32),
            jax.ShapeDtypeStruct((nodes, FOUR * LANES), bf16),
        ],
        scratch_shapes=[
            pltpu.VMEM((LANES, units), bf16),
            pltpu.VMEM((1, LANES), f32),
            pltpu.VMEM((LANES, nodes), f32),
        ],
        cost_estimate=pl.CostEstimate(
            flops=2 * FOUR * nodes * width * units, bytes_accessed=16 << 20, transcendentals=0
        ),
        name="forward",
    )(flat, w_in, b_in, wo_t, b_out, truth, area)


def cells_kernel(far_half, core_ref, cell_ref, pred_ref, out_ref):
    nodes = pred_ref.shape[0]
    half = core_ref[0] if not far_half else 1 - core_ref[0]
    ids = lax.broadcasted_iota(jnp.int32, (HALF, nodes), 0) + half * HALF
    picker = jnp.where(ids == cell_ref[...], 1.0, 0.0).astype(bf16)
    out_ref[...] = jnp.dot(picker, pred_ref[...], preferred_element_type=f32).astype(out_ref.dtype)


def cell_sums(core, cell, pred, far_half, dtype):
    return pl.pallas_call(
        functools.partial(cells_kernel, far_half),
        in_specs=[smem(), vmem(), vmem()],
        out_specs=vmem(),
        out_shape=jax.ShapeDtypeStruct((HALF, pred.shape[1]), dtype),
        compiler_params=fits(8),
        cost_estimate=pl.CostEstimate(
            flops=2 * HALF * pred.size, bytes_accessed=2 << 20, transcendentals=0
        ),
        name="cells",
    )(core, cell, pred)


def split_kernel(place_ref, pred_ref, *out_refs):
    for k, out_ref in enumerate(out_refs):
        out_ref[...] = pred_ref[(place_ref[0] + k) & 3]


def split(place, blocks):
    shape = jax.ShapeDtypeStruct(blocks.shape[1:], bf16)
    return pl.pallas_call(
        split_kernel,
        in_specs=[smem(), vmem()],
        out_specs=[vmem()] * FOUR,
        out_shape=[shape] * FOUR,
        compiler_params=fits(4),
        cost_estimate=pl.CostEstimate(flops=1 << 18, bytes_accessed=1 << 20, transcendentals=0),
        name="split",
    )(place, blocks)


def fine_kernel(place_ref, truth_ref, area_ref, *refs):
    got, grad, loss_ref, part, slope = refs[:4], refs[4:8], refs[8], refs[9], refs[10]
    for k in range(MEMBERS):
        block = got[k // FOUR][:, (k % FOUR) * LANES : (k % FOUR + 1) * LANES]
        part[k] = block.astype(f32).T[:VARS, :]
    start = pl.multiple_of(place_ref[0] * LANES, LANES)
    truth = truth_ref[:, pl.ds(start, LANES)]
    area = area_ref[:, pl.ds(start, LANES)]
    slope[:, VARS:, :] = jnp.zeros((MEMBERS, LANES - VARS, LANES), f32)

    def member(m, carry):
        truths, pairs = carry
        own = part[m]
        off = own - truth
        mean = jnp.sum(off * off, axis=0, keepdims=True) * (1.0 / VARS) + EPSILON
        inverse = lax.rsqrt(mean)
        truths = truths + mean * inverse
        total = jnp.zeros_like(own)
        for k in range(MEMBERS):
            between = own - part[k]
            mean = jnp.sum(between * between, axis=0, keepdims=True) * (1.0 / VARS) + EPSILON
            weight = lax.rsqrt(mean)
            distinct = jnp.where(m == k, 0.0, 1.0)
            pairs = pairs + (mean * weight) * distinct
            total = total + between * weight
        slope[m, :VARS, :] = off * (inverse * area * TRUTH_SCALE) - total * (area * PAIR_SCALE)
        return truths, pairs

    zero = jnp.zeros((1, LANES), f32)
    truths, pairs = lax.fori_loop(0, MEMBERS, member, (zero, zero))
    loss_ref[...] = area * (truths * (1.0 / MEMBERS) - pairs * (0.5 / PAIRS))
    for k in range(MEMBERS):
        grad[k // FOUR][:, (k % FOUR) * LANES : (k % FOUR + 1) * LANES] = slope[k].T.astype(bf16)


def fine(place, truth, area, got):
    shape = jax.ShapeDtypeStruct(got[0].shape, bf16)
    return pl.pallas_call(
        fine_kernel,
        in_specs=[smem()] + [vmem()] * 6,
        out_specs=[vmem()] * 5,
        out_shape=[shape] * FOUR + [jax.ShapeDtypeStruct((1, LANES), f32)],
        compiler_params=fits(10),
        scratch_shapes=[
            pltpu.VMEM((MEMBERS, VARS, LANES), f32),
            pltpu.VMEM((MEMBERS, LANES, LANES), f32),
        ],
        cost_estimate=pl.CostEstimate(
            flops=MEMBERS * MEMBERS * VARS * LANES * 16, bytes_accessed=2 << 20, transcendentals=0
        ),
        name="fine",
    )(place, truth, area, *got)


def three(value):
    high = value.astype(bf16).astype(f32)
    rest = value - high
    middle = rest.astype(bf16).astype(f32)
    return high, middle, rest - middle


def coarse_kernel(got_ref, loss_ref, area_ref, out_ref):
    places = got_ref.shape[0] // FOUR
    lane = lax.broadcasted_iota(jnp.int32, (8, LANES), 1)
    rank = lax.broadcasted_iota(jnp.int32, (8, LANES), 0)
    real = lane < VARS
    spare = lane >= VARS + 24
    sums = []
    for m in range(FOUR):
        total = got_ref[m].astype(f32)
        for s in range(1, places):
            total = total + got_ref[s * FOUR + m].astype(f32)
        sums += [total[:, j * LANES : (j + 1) * LANES] for j in range(FOUR)]

    def across(value):
        return jnp.sum(value, axis=1, keepdims=True)

    counts = across(jnp.where(spare, sums[0] + sums[1], 0.0))
    weight = across(jnp.where(spare, sums[2], 0.0))
    inverse = 1.0 / jnp.maximum(counts, 1.0)
    truth = jnp.zeros((8, LANES), f32)
    for j in range(FOUR):
        turned = pltpu.roll(sums[j], (24 * j - VARS) % LANES, 1)
        truth = jnp.where((lane >= 24 * j) & (lane < 24 * (j + 1)), turned, truth)
    truth = truth * inverse
    means = [jnp.where(real, (v * inverse).astype(bf16).astype(f32), 0.0) for v in sums]
    truths = jnp.zeros((8, 1), f32)
    pairs = jnp.zeros((8, 1), f32)
    grads = []
    for m in range(MEMBERS):
        off = means[m] - truth
        mean = across(off * off) * (1.0 / VARS) + EPSILON
        turn = lax.rsqrt(mean)
        truths = truths + mean * turn
        grads.append(off * (turn * TRUTH_SCALE))
    for m in range(MEMBERS):
        for k in range(m):
            between = means[m] - means[k]
            mean = across(between * between) * (1.0 / VARS) + EPSILON
            turn = lax.rsqrt(mean)
            pairs = pairs + mean * turn
            pull = between * (turn * PAIR_SCALE)
            grads[m] = grads[m] - pull
            grads[k] = grads[k] + pull
    loss = jnp.sum(weight * (truths * (1.0 / MEMBERS) - pairs * (1.0 / PAIRS)), axis=0, keepdims=True)
    fine_loss = across(loss_ref[...])
    area = across(area_ref[...])
    pieces = jnp.zeros((8, LANES), f32)
    for index, value in enumerate((*three(fine_loss), *three(loss), *three(area))):
        pieces = jnp.where(lane == VARS + index, value, pieces)
    pieces = jnp.where(rank == 0, pieces, 0.0)
    scale = weight * inverse
    for m in range(FOUR):
        rows = [grads[m * FOUR + j] * scale for j in range(FOUR)]
        rows[0] = rows[0] + pieces
        block = jnp.concatenate(rows, axis=1).astype(bf16)
        for s in range(places):
            out_ref[s * FOUR + m] = block


def coarse(got, loss, area):
    return pl.pallas_call(
        coarse_kernel,
        in_specs=[vmem(), vmem(), vmem()],
        out_specs=vmem(),
        out_shape=jax.ShapeDtypeStruct(got.shape, bf16),
        compiler_params=fits(6),
        cost_estimate=pl.CostEstimate(flops=1 << 21, bytes_accessed=1 << 20, transcendentals=0),
        name="coarse",
    )(got, loss, area)


def picked(half, column, table):
    first = (half * HALF).astype(f32)
    ids = lax.broadcasted_iota(jnp.int32, (column.shape[0], HALF), 1).astype(f32) + first
    wide = jnp.concatenate([column] * (HALF // LANES), axis=1)
    picker = jnp.where(ids == wide, 1.0, 0.0).astype(bf16)
    return jnp.dot(picker, table, preferred_element_type=f32)


def base_kernel(place_ref, cell_ref, *refs):
    got, base_ref, column_ref = refs[:4], refs[4], refs[5]
    nodes = cell_ref.shape[1]
    column_ref[...] = jnp.broadcast_to(cell_ref[...].astype(f32), (LANES, nodes)).T
    for k in range(FOUR):
        base_ref[(place_ref[0] + k) & 3] = got[k][...].astype(f32)


def based(place, cell, got):
    return pl.pallas_call(
        base_kernel,
        in_specs=[smem()] + [vmem()] * 5,
        out_specs=[vmem(), vmem()],
        out_shape=[
            jax.ShapeDtypeStruct((FOUR, *got[0].shape), f32),
            jax.ShapeDtypeStruct((cell.shape[1], LANES), f32),
        ],
        compiler_params=fits(6),
        cost_estimate=pl.CostEstimate(flops=1 << 20, bytes_accessed=2 << 20, transcendentals=0),
        name="base",
    )(place, cell, *got)


def near_kernel(core_ref, column_ref, base_ref, table_ref, out_ref):
    out_ref[...] = base_ref[...] + picked(core_ref[0], column_ref[...], table_ref[...])


def near(core, column, base, table):
    return pl.pallas_call(
        near_kernel,
        in_specs=[smem(), vmem(), vmem(), vmem()],
        out_specs=vmem(),
        out_shape=jax.ShapeDtypeStruct(base.shape, f32),
        compiler_params=fits(8),
        cost_estimate=pl.CostEstimate(
            flops=2 * HALF * table.size, bytes_accessed=2 << 20, transcendentals=0
        ),
        name="near",
    )(core, column, base, table)


def far_kernel(
    core_ref, column_ref, near_ref, own_ref, other_ref, up_ref, factor_ref, score_ref
):
    total = near_ref[...] + picked(1 - core_ref[0], column_ref[...], other_ref[...])
    up_ref[...] = total.astype(bf16)
    sums = own_ref[:, :LANES].astype(f32) + other_ref[:, :LANES].astype(f32)
    sums = jnp.sum(sums, axis=0, keepdims=True)
    lane = lax.broadcasted_iota(jnp.int32, (1, LANES), 1)

    def of(index):
        here = (lane >= VARS + 3 * index) & (lane < VARS + 3 * index + 3)
        return jnp.sum(jnp.where(here, sums, 0.0), axis=1, keepdims=True)

    area = of(2) * (1.0 / FOUR)
    factor_ref[...] = jnp.broadcast_to(LOSS_SCALE * NODE_TOTAL / area, (1, LANES))
    score_ref[0] = (of(0) / area)[0, 0]
    score_ref[1] = (of(1) / area)[0, 0]


def far(core, column, near_part, own, other):
    return pl.pallas_call(
        far_kernel,
        in_specs=[smem()] + [vmem()] * 4,
        out_specs=[vmem(), vmem(), smem()],
        compiler_params=fits(10),
        out_shape=[
            jax.ShapeDtypeStruct(near_part.shape, bf16),
            jax.ShapeDtypeStruct((1, LANES), f32),
            jax.ShapeDtypeStruct((2,), f32),
        ],
        name="far",
    )(core, column, near_part, own, other)


def backward_kernel(up_ref, preact_ref, wo_ref, w_ref, factor_ref, out_ref, wide, grads):
    @pl.when(pl.program_id(0) == 0)
    def _():
        wide[:VARS, :] = wo_ref[...]
        wide[VARS:, :] = jnp.zeros((LANES - VARS, wide.shape[1]), bf16)

    units = w_ref.shape[1]
    step = 256
    for n in range(0, units, step):
        hidden = jnp.dot(up_ref[...], wide[:, n : n + step], preferred_element_type=f32)
        pre = preact_ref[:, n : n + step]
        sigma = 0.5 * jnp.tanh(0.5 * pre) + 0.5
        slope = sigma * (1.0 + pre * (1.0 - sigma))
        grads[:, n : n + step] = (hidden * slope).astype(bf16)
    for n in range(0, w_ref.shape[0], step):
        total = lax.dot_general(
            grads[...], w_ref[n : n + step, :], (((1,), (1,)), ((), ())), preferred_element_type=f32
        )
        out_ref[:, n : n + step] = (total * factor_ref[0:1, 0:1]).astype(bf16)


def backward(up, preact, wo_t, w_in, factor, nodes):
    width, units = w_in.shape
    return pl.pallas_call(
        backward_kernel,
        grid=(FOUR,),
        in_specs=[
            pl.BlockSpec((nodes, LANES), lambda j: (0, j)),
            pl.BlockSpec((nodes, units), lambda j: (j, 0)),
            pl.BlockSpec((VARS, units), lambda j: (0, 0)),
            pl.BlockSpec((width, units), lambda j: (0, 0)),
            pl.BlockSpec((1, LANES), lambda j: (0, 0)),
        ],
        out_specs=pl.BlockSpec((nodes, width), lambda j: (j, 0)),
        out_shape=jax.ShapeDtypeStruct((FOUR * nodes, width), bf16),
        scratch_shapes=[pltpu.VMEM((LANES, units), bf16), pltpu.VMEM((nodes, units), bf16)],
        cost_estimate=pl.CostEstimate(
            flops=2 * FOUR * nodes * width * units, bytes_accessed=16 << 20, transcendentals=0
        ),
        name="backward",
    )(up, preact, wo_t, w_in, factor)


def turned(block, places):
    return lax.ppermute(block, "m", [(j, (j + places) % FOUR) for j in range(FOUR)])


def shards(latent, w_in, b_in, w_out, b_out, target, area, cell_of):
    members, nodes, width = latent.shape
    flat = latent.reshape(members * nodes, width)
    wo_t = w_out.T
    truth = target.T
    cell = cell_of[None, :]
    area_row = area[None, :]
    place = lax.axis_index("m").astype(jnp.int32)[None]
    core = lax.axis_index("c").astype(jnp.int32)[None]
    swap = [(0, 1), (1, 0)]

    preact, pred = forward(flat, w_in, b_in[None, :], wo_t, b_out[None, :], truth, area_row, nodes)
    sent = cell_sums(core, cell, pred, True, bf16)
    arrived = lax.ppermute(sent, "c", swap)
    blocks = split(place, pred.reshape(FOUR, LANES, FOUR * LANES))
    parts = [blocks[0]] + [turned(blocks[k], k) for k in range(1, FOUR)]
    kept = cell_sums(core, cell, pred, False, f32)
    both = (kept + arrived.astype(f32)).astype(bf16).reshape(64, 8, FOUR * LANES)
    gathered = lax.all_to_all(both, WIDE, 0, 0, tiled=True)
    *grads, fine_loss = fine(place, truth, area_row, parts)
    grads = [grads[0]] + [turned(grads[k], -k) for k in range(1, FOUR)]
    table = coarse(gathered, fine_loss, area_row)
    own = lax.all_to_all(table, WIDE, 0, 0, tiled=True)
    own = own.reshape(HALF, FOUR * LANES)
    base, column = based(place, cell, grads)
    other = lax.ppermute(own, "c", swap)
    near_part = near(core, column, base.reshape(nodes, FOUR * LANES), own)
    up, factor, scores = far(core, column, near_part, own, other)
    latent_grad = backward(up, preact, wo_t, w_in, factor, nodes)
    return (latent_grad.reshape(members, nodes, width), scores)


def solution(mesh):
    split = Mesh(mesh.devices.reshape(4, 4, 2, mesh.shape["member"]), ("x", "y", "c", "m"))
    return jax.shard_map(
        shards,
        mesh=split,
        in_specs=(P("m", SPACE, None), P(), P(), P(), P(), P(SPACE, None), P(SPACE), P(SPACE)),
        out_specs=(P("m", SPACE, None), P()),
        check_vma=False,
    )
```

```python
import jax
import jax.numpy as jnp
from jax import lax
from jax.experimental import pallas as pl
from jax.experimental.pallas import tpu as pltpu
from jax.sharding import Mesh
from jax.sharding import PartitionSpec as P

SPACE = ("x", "y", "c")
WIDE = ("x", "y", "m")

EPSILON = 1e-05
LOSS_SCALE = 4096.0
LANES = 128
VARS = 96
FOUR = 4
MEMBERS = 16
CELLS = 1024
HALF = CELLS // 2
NODE_TOTAL = 16384
PAIRS = float(MEMBERS * (MEMBERS - 1))
TRUTH_SCALE = 1.0 / (MEMBERS * VARS)
PAIR_SCALE = 1.0 / (PAIRS * VARS)

f32 = jnp.float32
bf16 = jnp.bfloat16


def vmem():
    return pl.BlockSpec(memory_space=pltpu.VMEM)


def fits(mib):
    return pltpu.CompilerParams(vmem_limit_bytes=mib << 20)


def in_hbm(value):
    return pltpu.with_memory_space_constraint(value, pltpu.HBM)


def smem():
    return pl.BlockSpec(memory_space=pltpu.SMEM)


def forward_kernel(
    x_ref, w_ref, b_ref, wo_ref, bo_ref, truth_ref, area_ref, cell_ref, slope_ref, pred_ref, wide, bias, extra
):
    j = pl.program_id(0)
    nodes = x_ref.shape[0]
    spare = LANES - VARS

    @pl.when(j == 0)
    def _():
        wide[:VARS, :] = wo_ref[...]
        wide[VARS:, :] = jnp.zeros((spare, wide.shape[1]), bf16)
        bias[...] = jnp.zeros_like(bias)
        bias[:, :VARS] = bo_ref[...]
        extra[:VARS, :] = jnp.zeros((VARS, nodes), f32)

    lane = lax.broadcasted_iota(jnp.int32, (8, nodes), 1)
    rank = lax.broadcasted_iota(jnp.int32, (8, nodes), 0)
    ones = jnp.where((lane & 15) == rank + 8 * j, 1.0, 0.0)
    spread = jnp.where((lane & 7) == rank, area_ref[...], 0.0)
    high, low = cell_ref[...] >> 5, cell_ref[...] & 31
    ids = jnp.where(rank == 0, high, jnp.where(rank == 1, low, 0)).astype(f32)
    features = jnp.where(j < 2, ones, jnp.where(j == 2, spread, ids))
    extra[VARS : VARS + 24, :] = truth_ref[pl.ds(pl.multiple_of(24 * j, 8), 24), :]
    extra[VARS + 24 :, :] = features
    pre = jnp.dot(x_ref[...], w_ref[...], preferred_element_type=f32) + b_ref[...]
    sigma = 0.5 * jnp.tanh(0.5 * pre) + 0.5
    silu = pre * sigma
    slope_ref[...] = (sigma + silu * (1.0 - sigma)).astype(bf16)
    act = silu.astype(bf16)
    total = lax.dot_general(act, wide[...], (((1,), (1,)), ((), ())), preferred_element_type=f32)
    pred_ref[...] = (total + bias[...] + extra[...].T).astype(bf16)


def forward(flat, w_in, b_in, wo_t, b_out, truth, area, cell, nodes):
    width, units = w_in.shape
    return pl.pallas_call(
        forward_kernel,
        grid=(FOUR,),
        in_specs=[
            pl.BlockSpec((nodes, width), lambda j: (j, 0)),
            pl.BlockSpec((width, units), lambda j: (0, 0)),
            pl.BlockSpec((1, units), lambda j: (0, 0)),
            pl.BlockSpec((VARS, units), lambda j: (0, 0)),
            pl.BlockSpec((1, VARS), lambda j: (0, 0)),
            pl.BlockSpec((VARS, nodes), lambda j: (0, 0)),
            pl.BlockSpec((1, nodes), lambda j: (0, 0)),
            pl.BlockSpec((1, nodes), lambda j: (0, 0)),
        ],
        out_specs=[
            pl.BlockSpec((nodes, units), lambda j: (j, 0)),
            pl.BlockSpec((nodes, LANES), lambda j: (0, j)),
        ],
        out_shape=[
            pltpu.HBM((FOUR * nodes, units), bf16),
            jax.ShapeDtypeStruct((nodes, FOUR * LANES), bf16),
        ],
        scratch_shapes=[
            pltpu.VMEM((LANES, units), bf16),
            pltpu.VMEM((1, LANES), f32),
            pltpu.VMEM((LANES, nodes), f32),
        ],
        compiler_params=fits(24),
        cost_estimate=pl.CostEstimate(
            flops=2 * FOUR * nodes * width * units, bytes_accessed=16 << 20, transcendentals=0
        ),
        name="forward",
    )(flat, w_in, b_in, wo_t, b_out, truth, area, cell)


def gathered_rows(core, ids, pred):
    here = lax.broadcasted_iota(jnp.int32, (HALF, pred.shape[0]), 0) + core * HALF
    picker = jnp.where(here == ids, 1.0, 0.0).astype(bf16)
    return jnp.dot(picker, pred, preferred_element_type=f32)


def ours_kernel(core_ref, cell_ref, pred_ref, out_ref):
    out_ref[...] = gathered_rows(core_ref[0], cell_ref[...], pred_ref[...])


def ours(core, cell, pred):
    return pl.pallas_call(
        ours_kernel,
        in_specs=[smem(), vmem(), vmem()],
        out_specs=vmem(),
        out_shape=jax.ShapeDtypeStruct((HALF, pred.shape[1]), f32),
        compiler_params=fits(8),
        cost_estimate=pl.CostEstimate(
            flops=2 * HALF * pred.size, bytes_accessed=2 << 20, transcendentals=0
        ),
        name="ours",
    )(core, cell, pred)


def theirs_kernel(core_ref, ours_ref, pred_ref, out_ref):
    lane = lax.broadcasted_iota(jnp.int32, (8, LANES), 1)
    digits = jnp.where(lane == VARS + 24, 32.0, jnp.where(lane == VARS + 25, 1.0, 0.0)).astype(bf16)
    last = pred_ref[:, (FOUR - 1) * LANES :]
    ids = lax.dot_general(digits, last, (((1,), (1,)), ((), ())), preferred_element_type=f32)
    ids = ids[0:1, :].astype(jnp.int32)
    total = ours_ref[...] + gathered_rows(core_ref[0], ids, pred_ref[...])
    out_ref[...] = total.astype(bf16)


def theirs(core, partial, pred):
    return pl.pallas_call(
        theirs_kernel,
        in_specs=[smem(), vmem(), vmem()],
        out_specs=vmem(),
        out_shape=jax.ShapeDtypeStruct(partial.shape, bf16),
        compiler_params=fits(8),
        cost_estimate=pl.CostEstimate(
            flops=2 * HALF * pred.size, bytes_accessed=2 << 20, transcendentals=0
        ),
        name="theirs",
    )(core, partial, pred)


def split_kernel(place_ref, pred_ref, *out_refs):
    for k, out_ref in enumerate(out_refs):
        out_ref[...] = pred_ref[(place_ref[0] + k) & 3]


def split(place, blocks):
    shape = jax.ShapeDtypeStruct(blocks.shape[1:], bf16)
    return pl.pallas_call(
        split_kernel,
        in_specs=[smem(), vmem()],
        out_specs=[vmem()] * FOUR,
        out_shape=[shape] * FOUR,
        compiler_params=fits(4),
        cost_estimate=pl.CostEstimate(flops=1 << 18, bytes_accessed=1 << 20, transcendentals=0),
        name="split",
    )(place, blocks)


def fine_kernel(place_ref, truth_ref, area_ref, *refs):
    got, grad, loss_ref, part, slope = refs[:4], refs[4:8], refs[8], refs[9], refs[10]
    for k in range(MEMBERS):
        block = got[k // FOUR][:, (k % FOUR) * LANES : (k % FOUR + 1) * LANES]
        part[k] = block.astype(f32).T[:VARS, :]
    start = pl.multiple_of(place_ref[0] * LANES, LANES)
    truth = truth_ref[:, pl.ds(start, LANES)]
    area = area_ref[:, pl.ds(start, LANES)]
    slope[...] = jnp.zeros((MEMBERS, LANES, LANES), f32)

    def member(m, pairs):
        own = part[m]
        total = slope[m, :VARS, :]
        for away in range(1, MEMBERS // 2 + 1):
            k = (m + away) & (MEMBERS - 1)
            between = own - part[k]
            mean = jnp.sum(between * between, axis=0, keepdims=True) * (1.0 / VARS) + EPSILON
            weight = lax.rsqrt(mean)
            pull = between * weight
            total = total + pull
            if away < MEMBERS // 2:
                slope[k, :VARS, :] = slope[k, :VARS, :] - pull
                pairs = pairs + mean * weight
            else:
                pairs = pairs + (0.5 * mean) * weight
        slope[m, :VARS, :] = total
        return pairs

    pairs = lax.fori_loop(0, MEMBERS, member, jnp.zeros((1, LANES), f32))
    truths = jnp.zeros((1, LANES), f32)
    for k in range(MEMBERS):
        off = part[k] - truth
        mean = jnp.sum(off * off, axis=0, keepdims=True) * (1.0 / VARS) + EPSILON
        inverse = lax.rsqrt(mean)
        truths = truths + mean * inverse
        own = off * (inverse * area * TRUTH_SCALE) - slope[k, :VARS, :] * (area * PAIR_SCALE)
        slope[k, :VARS, :] = own
        grad[k // FOUR][:, (k % FOUR) * LANES : (k % FOUR + 1) * LANES] = slope[k].T.astype(bf16)
    loss_ref[...] = area * (truths * (1.0 / MEMBERS) - pairs * (1.0 / PAIRS))


def fine(place, truth, area, got):
    shape = jax.ShapeDtypeStruct(got[0].shape, bf16)
    return pl.pallas_call(
        fine_kernel,
        in_specs=[smem()] + [vmem()] * 6,
        out_specs=[vmem()] * 5,
        out_shape=[shape] * FOUR + [jax.ShapeDtypeStruct((1, LANES), f32)],
        compiler_params=fits(10),
        scratch_shapes=[
            pltpu.VMEM((MEMBERS, VARS, LANES), f32),
            pltpu.VMEM((MEMBERS, LANES, LANES), f32),
        ],
        cost_estimate=pl.CostEstimate(
            flops=MEMBERS * MEMBERS * VARS * LANES * 16, bytes_accessed=2 << 20, transcendentals=0
        ),
        name="fine",
    )(place, truth, area, *got)


def three(value):
    high = value.astype(bf16).astype(f32)
    rest = value - high
    middle = rest.astype(bf16).astype(f32)
    return high, middle, rest - middle


def coarse_kernel(got_ref, loss_ref, area_ref, out_ref):
    places = got_ref.shape[0] // FOUR
    lane = lax.broadcasted_iota(jnp.int32, (8, LANES), 1)
    rank = lax.broadcasted_iota(jnp.int32, (8, LANES), 0)
    real = lane < VARS
    spare = lane >= VARS + 24
    sums = []
    for m in range(FOUR):
        total = got_ref[m].astype(f32)
        for s in range(1, places):
            total = total + got_ref[s * FOUR + m].astype(f32)
        sums += [total[:, j * LANES : (j + 1) * LANES] for j in range(FOUR)]

    def across(value):
        return jnp.sum(value, axis=1, keepdims=True)

    counts = across(jnp.where(spare, sums[0] + sums[1], 0.0))
    weight = across(jnp.where(spare, sums[2], 0.0))
    inverse = 1.0 / jnp.maximum(counts, 1.0)
    truth = jnp.zeros((8, LANES), f32)
    for j in range(FOUR):
        turned = pltpu.roll(sums[j], (24 * j - VARS) % LANES, 1)
        truth = jnp.where((lane >= 24 * j) & (lane < 24 * (j + 1)), turned, truth)
    truth = truth * inverse
    means = [jnp.where(real, (v * inverse).astype(bf16).astype(f32), 0.0) for v in sums]
    truths = jnp.zeros((8, 1), f32)
    pairs = jnp.zeros((8, 1), f32)
    grads = []
    for m in range(MEMBERS):
        off = means[m] - truth
        mean = across(off * off) * (1.0 / VARS) + EPSILON
        turn = lax.rsqrt(mean)
        truths = truths + mean * turn
        grads.append(off * (turn * TRUTH_SCALE))
    for m in range(MEMBERS):
        for k in range(m):
            between = means[m] - means[k]
            mean = across(between * between) * (1.0 / VARS) + EPSILON
            turn = lax.rsqrt(mean)
            pairs = pairs + mean * turn
            pull = between * (turn * PAIR_SCALE)
            grads[m] = grads[m] - pull
            grads[k] = grads[k] + pull
    loss = jnp.sum(weight * (truths * (1.0 / MEMBERS) - pairs * (1.0 / PAIRS)), axis=0, keepdims=True)
    fine_loss = across(loss_ref[...])
    area = across(area_ref[...])
    pieces = jnp.zeros((8, LANES), f32)
    for index, value in enumerate((*three(fine_loss), *three(loss), *three(area))):
        pieces = jnp.where(lane == VARS + index, value, pieces)
    pieces = jnp.where(rank == 0, pieces, 0.0)
    scale = weight * inverse
    for m in range(FOUR):
        rows = [grads[m * FOUR + j] * scale for j in range(FOUR)]
        rows[0] = rows[0] + pieces
        block = jnp.concatenate(rows, axis=1).astype(bf16)
        for s in range(places):
            out_ref[s * FOUR + m] = block


def coarse(got, loss, area):
    return pl.pallas_call(
        coarse_kernel,
        in_specs=[vmem(), vmem(), vmem()],
        out_specs=vmem(),
        out_shape=jax.ShapeDtypeStruct(got.shape, bf16),
        compiler_params=fits(6),
        cost_estimate=pl.CostEstimate(flops=1 << 21, bytes_accessed=1 << 20, transcendentals=0),
        name="coarse",
    )(got, loss, area)


def picked(half, column, table):
    first = (half * HALF).astype(f32)
    ids = lax.broadcasted_iota(jnp.int32, (column.shape[0], HALF), 1).astype(f32) + first
    wide = jnp.concatenate([column] * (HALF // LANES), axis=1)
    picker = jnp.where(ids == wide, 1.0, 0.0).astype(bf16)
    return jnp.dot(picker, table, preferred_element_type=f32)


def base_kernel(place_ref, cell_ref, *refs):
    got, base_ref, column_ref = refs[:4], refs[4], refs[5]
    nodes = cell_ref.shape[1]
    column_ref[...] = jnp.broadcast_to(cell_ref[...].astype(f32), (LANES, nodes)).T
    for k in range(FOUR):
        base_ref[(place_ref[0] + k) & 3] = got[k][...].astype(f32)


def based(place, cell, got):
    return pl.pallas_call(
        base_kernel,
        in_specs=[smem()] + [vmem()] * 5,
        out_specs=[vmem(), vmem()],
        out_shape=[
            jax.ShapeDtypeStruct((FOUR, *got[0].shape), f32),
            jax.ShapeDtypeStruct((cell.shape[1], LANES), f32),
        ],
        compiler_params=fits(6),
        cost_estimate=pl.CostEstimate(flops=1 << 20, bytes_accessed=2 << 20, transcendentals=0),
        name="base",
    )(place, cell, *got)


def near_kernel(core_ref, column_ref, base_ref, table_ref, out_ref):
    out_ref[...] = base_ref[...] + picked(core_ref[0], column_ref[...], table_ref[...])


def near(core, column, base, table):
    return pl.pallas_call(
        near_kernel,
        in_specs=[smem(), vmem(), vmem(), vmem()],
        out_specs=vmem(),
        out_shape=jax.ShapeDtypeStruct(base.shape, f32),
        compiler_params=fits(8),
        cost_estimate=pl.CostEstimate(
            flops=2 * HALF * table.size, bytes_accessed=2 << 20, transcendentals=0
        ),
        name="near",
    )(core, column, base, table)


def far_kernel(
    core_ref, column_ref, near_ref, own_ref, other_ref, up_ref, factor_ref, score_ref
):
    total = near_ref[...] + picked(1 - core_ref[0], column_ref[...], other_ref[...])
    up_ref[...] = total.astype(bf16)
    sums = own_ref[:, :LANES].astype(f32) + other_ref[:, :LANES].astype(f32)
    sums = jnp.sum(sums, axis=0, keepdims=True)
    lane = lax.broadcasted_iota(jnp.int32, (1, LANES), 1)

    def of(index):
        here = (lane >= VARS + 3 * index) & (lane < VARS + 3 * index + 3)
        return jnp.sum(jnp.where(here, sums, 0.0), axis=1, keepdims=True)

    area = of(2) * (1.0 / FOUR)
    factor_ref[...] = jnp.broadcast_to(LOSS_SCALE * NODE_TOTAL / area, (1, LANES))
    score_ref[0] = (of(0) / area)[0, 0]
    score_ref[1] = (of(1) / area)[0, 0]


def far(core, column, near_part, own, other):
    return pl.pallas_call(
        far_kernel,
        in_specs=[smem()] + [vmem()] * 4,
        out_specs=[vmem(), vmem(), smem()],
        compiler_params=fits(10),
        out_shape=[
            jax.ShapeDtypeStruct(near_part.shape, bf16),
            jax.ShapeDtypeStruct((1, LANES), f32),
            jax.ShapeDtypeStruct((2,), f32),
        ],
        name="far",
    )(core, column, near_part, own, other)


def backward_kernel(up_ref, slope_ref, wo_ref, w_ref, factor_ref, out_ref, wide, grads):
    @pl.when(pl.program_id(0) == 0)
    def _():
        wide[:VARS, :] = wo_ref[...]
        wide[VARS:, :] = jnp.zeros((LANES - VARS, wide.shape[1]), bf16)

    units = w_ref.shape[1]
    step = 256
    for n in range(0, units, step):
        hidden = jnp.dot(up_ref[...], wide[:, n : n + step], preferred_element_type=f32)
        slope = slope_ref[:, n : n + step].astype(f32)
        grads[:, n : n + step] = (hidden * slope).astype(bf16)
    for n in range(0, w_ref.shape[0], step):
        total = lax.dot_general(
            grads[...], w_ref[n : n + step, :], (((1,), (1,)), ((), ())), preferred_element_type=f32
        )
        out_ref[:, n : n + step] = (total * factor_ref[0:1, 0:1]).astype(bf16)


def backward(up, slope, wo_t, w_in, factor, nodes):
    width, units = w_in.shape
    return pl.pallas_call(
        backward_kernel,
        grid=(FOUR,),
        in_specs=[
            pl.BlockSpec((nodes, LANES), lambda j: (0, j)),
            pl.BlockSpec((nodes, units), lambda j: (j, 0)),
            pl.BlockSpec((VARS, units), lambda j: (0, 0)),
            pl.BlockSpec((width, units), lambda j: (0, 0)),
            pl.BlockSpec((1, LANES), lambda j: (0, 0)),
        ],
        out_specs=pl.BlockSpec((nodes, width), lambda j: (j, 0)),
        out_shape=jax.ShapeDtypeStruct((FOUR * nodes, width), bf16),
        scratch_shapes=[pltpu.VMEM((LANES, units), bf16), pltpu.VMEM((nodes, units), bf16)],
        compiler_params=fits(24),
        cost_estimate=pl.CostEstimate(
            flops=2 * FOUR * nodes * width * units, bytes_accessed=16 << 20, transcendentals=0
        ),
        name="backward",
    )(up, slope, wo_t, w_in, factor)


def turned(block, places):
    return lax.ppermute(block, "m", [(j, (j + places) % FOUR) for j in range(FOUR)])


def shards(latent, w_in, b_in, w_out, b_out, target, area, cell_of):
    members, nodes, width = latent.shape
    flat = latent.reshape(members * nodes, width)
    wo_t = w_out.T
    truth = target.T
    cell = cell_of[None, :]
    area_row = area[None, :]
    place = lax.axis_index("m").astype(jnp.int32)[None]
    core = lax.axis_index("c").astype(jnp.int32)[None]
    swap = [(0, 1), (1, 0)]

    inputs = (flat, w_in, b_in[None, :], wo_t, b_out[None, :], truth, area_row, cell)
    slope, pred = forward(*map(in_hbm, inputs), nodes)
    arrived = lax.ppermute(pred, "c", swap)
    blocks = split(place, pred.reshape(FOUR, LANES, FOUR * LANES))
    parts = [blocks[0]] + [turned(blocks[k], k) for k in range(1, FOUR)]
    both = theirs(core, ours(core, cell, pred), arrived).reshape(64, 8, FOUR * LANES)
    gathered = lax.all_to_all(both, WIDE, 0, 0, tiled=True)
    *grads, fine_loss = fine(place, truth, area_row, parts)
    grads = [grads[0]] + [turned(grads[k], -k) for k in range(1, FOUR)]
    table = coarse(gathered, fine_loss, area_row)
    own = lax.all_to_all(table, WIDE, 0, 0, tiled=True)
    own = own.reshape(HALF, FOUR * LANES)
    base, column = based(place, cell, grads)
    other = lax.ppermute(own, "c", swap)
    near_part = near(core, column, base.reshape(nodes, FOUR * LANES), own)
    up, factor, scores = far(core, column, near_part, own, other)
    latent_grad = backward(up, in_hbm(slope), wo_t, w_in, factor, nodes)
    return (latent_grad.reshape(members, nodes, width), scores)


def solution(mesh):
    split = Mesh(mesh.devices.reshape(4, 4, 2, mesh.shape["member"]), ("x", "y", "c", "m"))
    return jax.shard_map(
        shards,
        mesh=split,
        in_specs=(P("m", SPACE, None), P(), P(), P(), P(), P(SPACE, None), P(SPACE), P(SPACE)),
        out_specs=(P("m", SPACE, None), P()),
        check_vma=False,
    )
```

```python
import jax
import jax.numpy as jnp
from jax import lax
from jax.experimental import pallas as pl
from jax.experimental.pallas import tpu as pltpu
from jax.sharding import Mesh
from jax.sharding import PartitionSpec as P

SPACE = ("x", "y", "c")
WIDE = ("x", "y", "m")

EPSILON = 1e-05
LOSS_SCALE = 4096.0
LANES = 128
VARS = 96
FOUR = 4
MEMBERS = 16
CELLS = 1024
HALF = CELLS // 2
NODE_TOTAL = 16384
PAIRS = float(MEMBERS * (MEMBERS - 1))
TRUTH_SCALE = 1.0 / (MEMBERS * VARS)
PAIR_SCALE = 1.0 / (PAIRS * VARS)

f32 = jnp.float32
bf16 = jnp.bfloat16


def vmem():
    return pl.BlockSpec(memory_space=pltpu.VMEM)


def fits(mib):
    return pltpu.CompilerParams(vmem_limit_bytes=mib << 20)


def in_hbm(value):
    return pltpu.with_memory_space_constraint(value, pltpu.HBM)


def smem():
    return pl.BlockSpec(memory_space=pltpu.SMEM)


def forward_kernel(
    x_ref, w_ref, b_ref, wo_ref, bo_ref, truth_ref, area_ref, cell_ref, slope_ref, pred_ref, wide, bias, extra
):
    j = pl.program_id(0)
    nodes = x_ref.shape[0]
    spare = LANES - VARS

    @pl.when(j == 0)
    def _():
        wide[:VARS, :] = wo_ref[...]
        wide[VARS:, :] = jnp.zeros((spare, wide.shape[1]), bf16)
        bias[...] = jnp.zeros_like(bias)
        bias[:, :VARS] = bo_ref[...]
        extra[:VARS, :] = jnp.zeros((VARS, nodes), f32)

    lane = lax.broadcasted_iota(jnp.int32, (8, nodes), 1)
    rank = lax.broadcasted_iota(jnp.int32, (8, nodes), 0)
    ones = jnp.where((lane & 15) == rank + 8 * j, 1.0, 0.0)
    spread = jnp.where((lane & 7) == rank, area_ref[...], 0.0)
    high, low = cell_ref[...] >> 5, cell_ref[...] & 31
    ids = jnp.where(rank == 0, high, jnp.where(rank == 1, low, 0)).astype(f32)
    features = jnp.where(j < 2, ones, jnp.where(j == 2, spread, ids))
    extra[VARS : VARS + 24, :] = truth_ref[pl.ds(pl.multiple_of(24 * j, 8), 24), :]
    extra[VARS + 24 :, :] = features
    turned_extra = extra[...].T
    halves = 2
    rows = nodes // halves
    products = [
        jnp.dot(x_ref[k * rows : (k + 1) * rows, :], w_ref[...], preferred_element_type=f32)
        for k in range(halves)
    ]
    for k in range(halves):
        here = slice(k * rows, (k + 1) * rows)
        pre = products[k] + b_ref[...]
        sigma = 0.5 * jnp.tanh(0.5 * pre) + 0.5
        silu = pre * sigma
        slope_ref[here, :] = (sigma + silu * (1.0 - sigma)).astype(bf16)
        act = silu.astype(bf16)
        total = lax.dot_general(act, wide[...], (((1,), (1,)), ((), ())), preferred_element_type=f32)
        pred_ref[here, :] = (total + bias[...] + turned_extra[here, :]).astype(bf16)


def forward(flat, w_in, b_in, wo_t, b_out, truth, area, cell, nodes):
    width, units = w_in.shape
    return pl.pallas_call(
        forward_kernel,
        grid=(FOUR,),
        in_specs=[
            pl.BlockSpec((nodes, width), lambda j: (j, 0)),
            pl.BlockSpec((width, units), lambda j: (0, 0)),
            pl.BlockSpec((1, units), lambda j: (0, 0)),
            pl.BlockSpec((VARS, units), lambda j: (0, 0)),
            pl.BlockSpec((1, VARS), lambda j: (0, 0)),
            pl.BlockSpec((VARS, nodes), lambda j: (0, 0)),
            pl.BlockSpec((1, nodes), lambda j: (0, 0)),
            pl.BlockSpec((1, nodes), lambda j: (0, 0)),
        ],
        out_specs=[
            pl.BlockSpec((nodes, units), lambda j: (j, 0)),
            pl.BlockSpec((nodes, LANES), lambda j: (0, j)),
        ],
        out_shape=[
            pltpu.HBM((FOUR * nodes, units), bf16),
            jax.ShapeDtypeStruct((nodes, FOUR * LANES), bf16),
        ],
        scratch_shapes=[
            pltpu.VMEM((LANES, units), bf16),
            pltpu.VMEM((1, LANES), f32),
            pltpu.VMEM((LANES, nodes), f32),
        ],
        compiler_params=fits(24),
        cost_estimate=pl.CostEstimate(
            flops=2 * FOUR * nodes * width * units, bytes_accessed=16 << 20, transcendentals=0
        ),
        name="forward",
    )(flat, w_in, b_in, wo_t, b_out, truth, area, cell)


def gathered_rows(core, ids, pred):
    here = lax.broadcasted_iota(jnp.int32, (HALF, pred.shape[0]), 0) + core * HALF
    picker = jnp.where(here == ids, 1.0, 0.0).astype(bf16)
    return jnp.dot(picker, pred, preferred_element_type=f32)


def cells_kernel(core_ref, cell_ref, pred_ref, other_ref, out_ref):
    lane = lax.broadcasted_iota(jnp.int32, (8, LANES), 1)
    digits = jnp.where(lane == VARS + 24, 32.0, jnp.where(lane == VARS + 25, 1.0, 0.0)).astype(bf16)
    last = other_ref[:, (FOUR - 1) * LANES :]
    ids = lax.dot_general(digits, last, (((1,), (1,)), ((), ())), preferred_element_type=f32)
    ids = ids[0:1, :].astype(jnp.int32)
    core = core_ref[0]
    total = gathered_rows(core, cell_ref[...], pred_ref[...])
    out_ref[...] = (total + gathered_rows(core, ids, other_ref[...])).astype(bf16)


def cell_sums(core, cell, pred, other):
    return pl.pallas_call(
        cells_kernel,
        in_specs=[smem(), vmem(), vmem(), vmem()],
        out_specs=vmem(),
        out_shape=jax.ShapeDtypeStruct((HALF, pred.shape[1]), bf16),
        compiler_params=fits(8),
        cost_estimate=pl.CostEstimate(
            flops=4 * HALF * pred.size, bytes_accessed=2 << 20, transcendentals=0
        ),
        name="cells",
    )(core, cell, pred, other)


def split_kernel(place_ref, pred_ref, *out_refs):
    for k, out_ref in enumerate(out_refs):
        out_ref[...] = pred_ref[(place_ref[0] + k) & 3]


def split(place, blocks):
    shape = jax.ShapeDtypeStruct(blocks.shape[1:], bf16)
    return pl.pallas_call(
        split_kernel,
        in_specs=[smem(), vmem()],
        out_specs=[vmem()] * FOUR,
        out_shape=[shape] * FOUR,
        compiler_params=fits(4),
        cost_estimate=pl.CostEstimate(flops=1 << 18, bytes_accessed=1 << 20, transcendentals=0),
        name="split",
    )(place, blocks)


def fine_kernel(place_ref, truth_ref, area_ref, *refs):
    got, grad, loss_ref, part, slope = refs[:4], refs[4:8], refs[8], refs[9], refs[10]
    for k in range(MEMBERS):
        block = got[k // FOUR][:, (k % FOUR) * LANES : (k % FOUR + 1) * LANES]
        part[k] = block.astype(f32).T[:VARS, :]
    start = pl.multiple_of(place_ref[0] * LANES, LANES)
    truth = truth_ref[:, pl.ds(start, LANES)]
    area = area_ref[:, pl.ds(start, LANES)]
    slope[...] = jnp.zeros((MEMBERS, LANES, LANES), f32)

    def member(m, pairs):
        own = part[m]
        total = slope[m, :VARS, :]
        for away in range(1, MEMBERS // 2 + 1):
            k = (m + away) & (MEMBERS - 1)
            between = own - part[k]
            mean = jnp.sum(between * between, axis=0, keepdims=True) * (1.0 / VARS) + EPSILON
            weight = lax.rsqrt(mean)
            pull = between * weight
            total = total + pull
            if away < MEMBERS // 2:
                slope[k, :VARS, :] = slope[k, :VARS, :] - pull
                pairs = pairs + mean * weight
            else:
                pairs = pairs + (0.5 * mean) * weight
        slope[m, :VARS, :] = total
        return pairs

    pairs = lax.fori_loop(0, MEMBERS, member, jnp.zeros((1, LANES), f32))
    truths = jnp.zeros((1, LANES), f32)
    for k in range(MEMBERS):
        off = part[k] - truth
        mean = jnp.sum(off * off, axis=0, keepdims=True) * (1.0 / VARS) + EPSILON
        inverse = lax.rsqrt(mean)
        truths = truths + mean * inverse
        own = off * (inverse * area * TRUTH_SCALE) - slope[k, :VARS, :] * (area * PAIR_SCALE)
        slope[k, :VARS, :] = own
        grad[k // FOUR][:, (k % FOUR) * LANES : (k % FOUR + 1) * LANES] = slope[k].T.astype(bf16)
    loss_ref[...] = area * (truths * (1.0 / MEMBERS) - pairs * (1.0 / PAIRS))


def fine(place, truth, area, got):
    shape = jax.ShapeDtypeStruct(got[0].shape, bf16)
    return pl.pallas_call(
        fine_kernel,
        in_specs=[smem()] + [vmem()] * 6,
        out_specs=[vmem()] * 5,
        out_shape=[shape] * FOUR + [jax.ShapeDtypeStruct((1, LANES), f32)],
        compiler_params=fits(10),
        scratch_shapes=[
            pltpu.VMEM((MEMBERS, VARS, LANES), f32),
            pltpu.VMEM((MEMBERS, LANES, LANES), f32),
        ],
        cost_estimate=pl.CostEstimate(
            flops=MEMBERS * MEMBERS * VARS * LANES * 16, bytes_accessed=2 << 20, transcendentals=0
        ),
        name="fine",
    )(place, truth, area, *got)


def three(value):
    high = value.astype(bf16).astype(f32)
    rest = value - high
    middle = rest.astype(bf16).astype(f32)
    return high, middle, rest - middle


def coarse_kernel(got_ref, loss_ref, area_ref, out_ref):
    places = got_ref.shape[0] // FOUR
    lane = lax.broadcasted_iota(jnp.int32, (8, LANES), 1)
    rank = lax.broadcasted_iota(jnp.int32, (8, LANES), 0)
    real = lane < VARS
    spare = lane >= VARS + 24
    sums = []
    for m in range(FOUR):
        total = got_ref[m].astype(f32)
        for s in range(1, places):
            total = total + got_ref[s * FOUR + m].astype(f32)
        sums += [total[:, j * LANES : (j + 1) * LANES] for j in range(FOUR)]

    def across(value):
        return jnp.sum(value, axis=1, keepdims=True)

    counts = across(jnp.where(spare, sums[0] + sums[1], 0.0))
    weight = across(jnp.where(spare, sums[2], 0.0))
    inverse = 1.0 / jnp.maximum(counts, 1.0)
    truth = jnp.zeros((8, LANES), f32)
    for j in range(FOUR):
        turned = pltpu.roll(sums[j], (24 * j - VARS) % LANES, 1)
        truth = jnp.where((lane >= 24 * j) & (lane < 24 * (j + 1)), turned, truth)
    truth = truth * inverse
    means = [jnp.where(real, (v * inverse).astype(bf16).astype(f32), 0.0) for v in sums]
    truths = jnp.zeros((8, 1), f32)
    pairs = jnp.zeros((8, 1), f32)
    grads = []
    for m in range(MEMBERS):
        off = means[m] - truth
        mean = across(off * off) * (1.0 / VARS) + EPSILON
        turn = lax.rsqrt(mean)
        truths = truths + mean * turn
        grads.append(off * (turn * TRUTH_SCALE))
    for m in range(MEMBERS):
        for k in range(m):
            between = means[m] - means[k]
            mean = across(between * between) * (1.0 / VARS) + EPSILON
            turn = lax.rsqrt(mean)
            pairs = pairs + mean * turn
            pull = between * (turn * PAIR_SCALE)
            grads[m] = grads[m] - pull
            grads[k] = grads[k] + pull
    loss = jnp.sum(weight * (truths * (1.0 / MEMBERS) - pairs * (1.0 / PAIRS)), axis=0, keepdims=True)
    fine_loss = across(loss_ref[...])
    area = across(area_ref[...])
    pieces = jnp.zeros((8, LANES), f32)
    for index, value in enumerate((*three(fine_loss), *three(loss), *three(area))):
        pieces = jnp.where(lane == VARS + index, value, pieces)
    pieces = jnp.where(rank == 0, pieces, 0.0)
    scale = weight * inverse
    for m in range(FOUR):
        rows = [grads[m * FOUR + j] * scale for j in range(FOUR)]
        rows[0] = rows[0] + pieces
        block = jnp.concatenate(rows, axis=1).astype(bf16)
        for s in range(places):
            out_ref[s * FOUR + m] = block


def coarse(got, loss, area):
    return pl.pallas_call(
        coarse_kernel,
        in_specs=[vmem(), vmem(), vmem()],
        out_specs=vmem(),
        out_shape=jax.ShapeDtypeStruct(got.shape, bf16),
        compiler_params=fits(6),
        cost_estimate=pl.CostEstimate(flops=1 << 21, bytes_accessed=1 << 20, transcendentals=0),
        name="coarse",
    )(got, loss, area)


def base_kernel(place_ref, core_ref, cell_ref, *refs):
    got, base_ref, near_ref, far_ref = refs[:4], refs[4], refs[5], refs[6]
    nodes = cell_ref.shape[1]
    column = jnp.broadcast_to(cell_ref[...].astype(f32), (LANES, nodes)).T
    wide = jnp.concatenate([column] * (HALF // LANES), axis=1)
    for picker_ref, half in ((near_ref, core_ref[0]), (far_ref, 1 - core_ref[0])):
        ids = (lax.broadcasted_iota(jnp.int32, (nodes, HALF), 1) + half * HALF).astype(f32)
        picker_ref[...] = jnp.where(ids == wide, 1.0, 0.0).astype(bf16)
    for k in range(FOUR):
        base_ref[(place_ref[0] + k) & 3] = got[k][...].astype(f32)


def based(place, core, cell, got):
    return pl.pallas_call(
        base_kernel,
        in_specs=[smem(), smem()] + [vmem()] * 5,
        out_specs=[vmem()] * 3,
        out_shape=[
            jax.ShapeDtypeStruct((FOUR, *got[0].shape), f32),
            jax.ShapeDtypeStruct((cell.shape[1], HALF), bf16),
            jax.ShapeDtypeStruct((cell.shape[1], HALF), bf16),
        ],
        compiler_params=fits(8),
        cost_estimate=pl.CostEstimate(flops=1 << 20, bytes_accessed=2 << 20, transcendentals=0),
        name="base",
    )(place, core, cell, *got)


def spare_sums(table_ref):
    return jnp.sum(table_ref[:, :LANES].astype(f32), axis=0, keepdims=True)


def near_kernel(picker_ref, base_ref, table_ref, out_ref, sums_ref):
    picked = jnp.dot(picker_ref[...], table_ref[...], preferred_element_type=f32)
    out_ref[...] = base_ref[...] + picked
    sums_ref[...] = spare_sums(table_ref)


def near(picker, base, table):
    return pl.pallas_call(
        near_kernel,
        in_specs=[vmem()] * 3,
        out_specs=[vmem()] * 2,
        out_shape=[
            jax.ShapeDtypeStruct(base.shape, f32),
            jax.ShapeDtypeStruct((1, LANES), f32),
        ],
        compiler_params=fits(8),
        cost_estimate=pl.CostEstimate(
            flops=2 * HALF * table.size, bytes_accessed=2 << 20, transcendentals=0
        ),
        name="near",
    )(picker, base, table)


def far_kernel(picker_ref, near_ref, near_sums_ref, table_ref, up_ref, sums_ref):
    picked = jnp.dot(picker_ref[...], table_ref[...], preferred_element_type=f32)
    up_ref[...] = (near_ref[...] + picked).astype(bf16)
    sums_ref[...] = near_sums_ref[...] + spare_sums(table_ref)


def far(picker, near_part, near_sums, table):
    return pl.pallas_call(
        far_kernel,
        in_specs=[vmem()] * 4,
        out_specs=[vmem(), vmem()],
        compiler_params=fits(8),
        out_shape=[
            jax.ShapeDtypeStruct(near_part.shape, bf16),
            jax.ShapeDtypeStruct((1, LANES), f32),
        ],
        name="far",
    )(picker, near_part, near_sums, table)


def backward_kernel(up_ref, slope_ref, wo_ref, w_ref, sums_ref, out_ref, score_ref, wide, grads):
    sums = sums_ref[...]
    lane = lax.broadcasted_iota(jnp.int32, (1, LANES), 1)

    def of(index):
        here = (lane >= VARS + 3 * index) & (lane < VARS + 3 * index + 3)
        return jnp.sum(jnp.where(here, sums, 0.0), axis=1, keepdims=True)

    area = of(2) * (1.0 / FOUR)
    factor = LOSS_SCALE * NODE_TOTAL / area

    @pl.when(pl.program_id(0) == 0)
    def _():
        score_ref[0] = (of(0) / area)[0, 0]
        score_ref[1] = (of(1) / area)[0, 0]
        wide[:VARS, :] = wo_ref[...]
        wide[VARS:, :] = jnp.zeros((LANES - VARS, wide.shape[1]), bf16)

    units = w_ref.shape[1]
    step = 256
    for n in range(0, units, step):
        hidden = jnp.dot(up_ref[...], wide[:, n : n + step], preferred_element_type=f32)
        slope = slope_ref[:, n : n + step].astype(f32)
        grads[:, n : n + step] = (hidden * slope).astype(bf16)
    for n in range(0, w_ref.shape[0], step):
        total = lax.dot_general(
            grads[...], w_ref[n : n + step, :], (((1,), (1,)), ((), ())), preferred_element_type=f32
        )
        out_ref[:, n : n + step] = (total * factor).astype(bf16)


def backward(up, slope, wo_t, w_in, sums, nodes):
    width, units = w_in.shape
    return pl.pallas_call(
        backward_kernel,
        grid=(FOUR,),
        in_specs=[
            pl.BlockSpec((nodes, LANES), lambda j: (0, j)),
            pl.BlockSpec((nodes, units), lambda j: (j, 0)),
            pl.BlockSpec((VARS, units), lambda j: (0, 0)),
            pl.BlockSpec((width, units), lambda j: (0, 0)),
            pl.BlockSpec((1, LANES), lambda j: (0, 0)),
        ],
        out_specs=[pl.BlockSpec((nodes, width), lambda j: (j, 0)), smem()],
        out_shape=[
            jax.ShapeDtypeStruct((FOUR * nodes, width), bf16),
            jax.ShapeDtypeStruct((2,), f32),
        ],
        scratch_shapes=[pltpu.VMEM((LANES, units), bf16), pltpu.VMEM((nodes, units), bf16)],
        compiler_params=fits(24),
        cost_estimate=pl.CostEstimate(
            flops=2 * FOUR * nodes * width * units, bytes_accessed=16 << 20, transcendentals=0
        ),
        name="backward",
    )(up, slope, wo_t, w_in, sums)


def turned(block, places):
    return lax.ppermute(block, "m", [(j, (j + places) % FOUR) for j in range(FOUR)])


def shards(latent, w_in, b_in, w_out, b_out, target, area, cell_of):
    members, nodes, width = latent.shape
    flat = latent.reshape(members * nodes, width)
    wo_t = w_out.T
    truth = target.T
    cell = cell_of[None, :]
    area_row = area[None, :]
    place = lax.axis_index("m").astype(jnp.int32)[None]
    core = lax.axis_index("c").astype(jnp.int32)[None]
    swap = [(0, 1), (1, 0)]

    inputs = (flat, w_in, b_in[None, :], wo_t, b_out[None, :], truth, area_row, cell)
    slope, pred = forward(*map(in_hbm, inputs), nodes)
    arrived = lax.ppermute(pred, "c", swap)
    blocks = split(place, pred.reshape(FOUR, LANES, FOUR * LANES))
    parts = [blocks[0]] + [turned(blocks[k], k) for k in range(1, FOUR)]
    both = cell_sums(core, cell, pred, arrived).reshape(64, 8, FOUR * LANES)
    gathered = lax.all_to_all(both, WIDE, 0, 0, tiled=True)
    *grads, fine_loss = fine(place, truth, area_row, parts)
    grads = [grads[0]] + [turned(grads[k], -k) for k in range(1, FOUR)]
    table = coarse(gathered, fine_loss, area_row)
    own = lax.all_to_all(table, WIDE, 0, 0, tiled=True)
    own = own.reshape(HALF, FOUR * LANES)
    base, near_picker, far_picker = based(place, core, cell, grads)
    other = lax.ppermute(own, "c", swap)
    near_part, near_sums = near(near_picker, base.reshape(nodes, FOUR * LANES), own)
    up, sums = far(far_picker, near_part, near_sums, other)
    latent_grad, scores = backward(up, in_hbm(slope), wo_t, w_in, sums, nodes)
    return (latent_grad.reshape(members, nodes, width), scores)


def solution(mesh):
    split = Mesh(mesh.devices.reshape(4, 4, 2, mesh.shape["member"]), ("x", "y", "c", "m"))
    return jax.shard_map(
        shards,
        mesh=split,
        in_specs=(P("m", SPACE, None), P(), P(), P(), P(), P(SPACE, None), P(SPACE), P(SPACE)),
        out_specs=(P("m", SPACE, None), P()),
        check_vma=False,
    )
```
